32 devices in a mesh: fsdp: 8 (over z, x), rep: 4 (over y, core).
Axes of the slice: x: 2, y: 2, z: 4, core: 2. Of those that a mesh axis runs over, the one named last changes fastest.
Arguments:
- hidden_in: bfloat16 [16384, 768], P(('fsdp', 'rep')), may hold values from -6 to 6
- cotangent: bfloat16 [16384, 768], P(('fsdp', 'rep')), may hold values from -6 to 6
- lengths: int32 [32], P(('fsdp', 'rep')), may hold values from 1 to 512, as said below
- norm_gain: bfloat16 [768], P('fsdp'), may hold values from 0.5 to 1.5
- in_weight: bfloat16 [768, 3352], P('fsdp'), may hold values from -0.21875 to 0.21875
- conv_weight: bfloat16 [4, 1792], P(None, 'fsdp'), may hold values from -3 to 3
- conv_bias: bfloat16 [1792], P('fsdp'), may hold values from -2 to 2
- step_bias: float32 [24], replicated, may hold values from -6 to -2
- decay_log: float32 [24], replicated, may hold values from 0 to 2.77
- skip_weight: float32 [24], replicated, may hold values from 0.5 to 1.5
- mix_gain: bfloat16 [1536], P('fsdp'), may hold values from 0.5 to 1.5
- out_weight: bfloat16 [1536, 768], P('fsdp'), may hold values from -0.15625 to 0.15625
Outputs:
- block_out: bfloat16 [16384, 768], P(('fsdp', 'rep'))
- grad_in: float32 [16384, 768], P(('fsdp', 'rep'))
- grad_norm_gain: float32 [768], P('fsdp')
- grad_in_weight: float32 [768, 3352], P('fsdp')
- grad_conv_weight: float32 [4, 1792], P(None, 'fsdp')
- grad_conv_bias: float32 [1792], P('fsdp')
- grad_step_bias: float32 [24], replicated
- grad_decay_log: float32 [24], replicated
- grad_skip_weight: float32 [24], replicated
- grad_mix_gain: float32 [1536], P('fsdp')
- grad_out_weight: float32 [1536, 768], P('fsdp')
The draws below stay inside these ranges and needn't reach their ends.
Inputs may be any that keep to these rules, and one draw needn't show every extreme that they name: lengths[s] is the number of live tokens of sequence s, which fill its first slots; some sequence has 512 live tokens.
All inputs are finite; a program needn't handle non-finite values.
Results may differ from the reference program's by a relative error of at most 0.0068.
Values may be sent and summed in bfloat16 or wider, within the bound.
A program may use at most 192 MiB of HBM per device.

```python
import jax
import jax.numpy as jnp
from jax import lax

D = 768
NH = 24
HD = 64
NS = 128
KCONV = 4
SEQ_LEN = 512
DI = 1536
CONV_CH = 1792
PROJ = 3352
SEQS = 32
TOKENS = 16384


def draw_lengths(key, part):
    first_key, second_key, third_key = jax.random.split(jax.random.fold_in(key, 17), 3)
    first = jax.random.randint(first_key, (SEQS,), 1, SEQ_LEN + 1)
    second = jax.random.randint(second_key, (SEQS,), 1, SEQ_LEN + 1)
    picked = jax.random.randint(third_key, (), 0, SEQS)
    counts = jnp.minimum(first, second)
    counts = jnp.where(jnp.arange(SEQS) == picked, SEQ_LEN, counts)
    return counts.astype(jnp.int32)


def block_levels(key, shape, cuts, low, top_value):
    def one(dim, blocks):
        steps = jax.random.uniform(jax.random.fold_in(jax.random.fold_in(key, 6), dim), (blocks,), jnp.float32, low / len(cuts), top_value / len(cuts))
        return jnp.repeat(jnp.exp(steps), shape[dim] // blocks).reshape((-1,) + (1,) * (len(shape) - dim - 1))

    level = one(*cuts[0])
    for cut in cuts[1:]:
        level = level * one(*cut)
    return level


def bell_draw(key, dims, scale, most, cuts=(), kind=jnp.bfloat16):
    array = jax.random.normal(key, dims, jnp.float32) * scale
    if len(cuts) > 0:
        array = block_levels(key, dims, cuts, -0.22, 0.18) * array
    return jnp.clip(array, min=-most, max=most).astype(kind)


def setup_inputs(seed: int = 0) -> dict:
    streams_of = jax.random.split(jax.random.key(seed), 13)
    return {
        "hidden_in": bell_draw(streams_of[0], (TOKENS, D), 1.0, 6.0, ((0, 32),)),
        "cotangent": bell_draw(streams_of[1], (TOKENS, D), 1.0, 6.0, ((0, 32),)),
        "lengths": draw_lengths(jax.random.fold_in(streams_of[12], 71), 0),
        "norm_gain": jnp.clip(1.0 + 0.1 * jax.random.normal(streams_of[3], (D,), jnp.float32), 0.5, 1.5).astype(jnp.bfloat16),
        "in_weight": bell_draw(streams_of[4], (D, PROJ), D ** -0.5, 0.21875, ((0, 8),)),
        "conv_weight": bell_draw(streams_of[5], (KCONV, CONV_CH), 0.5, 3.0, ((1, 8),)),
        "conv_bias": bell_draw(streams_of[6], (CONV_CH,), 0.3, 2.0, ((0, 8),)),
        "step_bias": jnp.clip(jax.random.uniform(streams_of[7], (NH,), jnp.float32, -6.0, -2.0), -6.0, -2.0),
        "decay_log": jnp.clip(jax.random.uniform(streams_of[8], (NH,), jnp.float32, 0.0, 2.77), 0.0, 2.77),
        "skip_weight": jnp.clip(jax.random.uniform(streams_of[9], (NH,), jnp.float32, 0.5, 1.5), 0.5, 1.5),
        "mix_gain": jnp.clip(1.0 + 0.1 * jax.random.normal(streams_of[10], (DI,), jnp.float32), 0.5, 1.5).astype(jnp.bfloat16),
        "out_weight": bell_draw(streams_of[11], (DI, D), DI ** -0.5, 0.15625, ((0, 8),)),
    }


EPS = 1e-05
HIGH = lax.Precision.HIGHEST

def pre_norm(rows, gain):
    scale = lax.rsqrt(lax.optimization_barrier(jnp.mean(rows * rows, axis=-1, keepdims=True)) + EPS)
    return rows * scale * gain

def quadratic_scan(values, step, logdecay, keys_b, query_c):
    length = values.shape[1]
    cumlog = jnp.cumsum(logdecay, axis=1)
    spread = cumlog[:, :, None, :] - cumlog[:, None, :, :]
    causal = (jnp.arange(length)[:, None] >= jnp.arange(length)[None, :])[None, :, :, None]
    decay = jnp.exp(jnp.where(causal, spread, -jnp.inf))
    intersection = jnp.einsum('stn,sun->stu', query_c, keys_b, precision=HIGH)
    scaled = values * step[..., None]
    return jnp.einsum('stuh,suhp->sthp', intersection[..., None] * decay, scaled, precision=HIGH)

def mixer_core(proj, conv_w, conv_b, step_bias, decay_log, skip_weight, mix_gain, scan_fn):
    seqs_here = proj.shape[0]
    length = proj.shape[1]
    gate = proj[..., :DI]
    conv_in = proj[..., DI:DI + CONV_CH]
    step_raw = proj[..., DI + CONV_CH:]
    padded = jnp.pad(conv_in, ((0, 0), (KCONV - 1, 0), (0, 0)))
    conv_out = jnp.zeros_like(conv_in) + conv_b
    for offset in range(KCONV):
        conv_out = conv_out + conv_w[offset] * padded[:, offset:offset + length]
    active = jax.nn.silu(conv_out)
    values = active[..., :DI].reshape(seqs_here, length, NH, HD)
    keys_b = active[..., DI:DI + NS]
    query_c = active[..., DI + NS:]
    step = jax.nn.softplus(step_raw + step_bias)
    logdecay = -step * jnp.exp(decay_log)
    mixed = scan_fn(values, step, logdecay, keys_b, query_c)
    mixed = mixed + skip_weight[:, None] * values
    flat = mixed.reshape(seqs_here, length, DI) * jax.nn.silu(gate)
    scale = lax.rsqrt(lax.optimization_barrier(jnp.mean(flat * flat, axis=-1, keepdims=True)) + EPS)
    return flat * scale * mix_gain

def reference(hidden_in, cotangent, lengths, norm_gain, in_weight, conv_weight, conv_bias, step_bias, decay_log, skip_weight, mix_gain, out_weight):
    gain_one = norm_gain.astype(jnp.float32)
    conv_w = conv_weight.astype(jnp.float32)
    conv_b = conv_bias.astype(jnp.float32)
    mix_full = mix_gain.astype(jnp.float32)
    rows_all = hidden_in.reshape(SEQS, SEQ_LEN, D)
    cots_all = cotangent.reshape(SEQS, SEQ_LEN, D)

    def core(proj, cw, cb, sb, dl, sk, mg):
        return mixer_core(proj[None], cw, cb, sb, dl, sk, mg, quadratic_scan)[0]

    def one_seq(carry, item):
        rows, cots, count = item
        resid = rows.astype(jnp.float32)
        normed, norm_back = jax.vjp(pre_norm, resid, gain_one)
        normed_b = normed.astype(jnp.bfloat16)
        proj = jnp.dot(normed_b, in_weight, preferred_element_type=jnp.float32)
        gated, core_back = jax.vjp(core, proj, conv_w, conv_b, step_bias, decay_log, skip_weight, mix_full)
        gated_b = gated.astype(jnp.bfloat16)
        branch = jnp.dot(gated_b, out_weight, preferred_element_type=jnp.float32)
        live = (jnp.arange(SEQ_LEN) < count).astype(jnp.float32)[:, None]
        out_rows = (resid + live * branch).astype(jnp.bfloat16)
        cot_live = cots * live.astype(jnp.bfloat16)
        d_gated = jnp.dot(cot_live, out_weight.T, preferred_element_type=jnp.float32)
        d_out_w = jnp.dot(gated_b.T, cot_live, preferred_element_type=jnp.float32)
        d_proj, d_cw, d_cb, d_sb, d_dl, d_sk, d_mg = core_back(d_gated)
        d_proj_b = d_proj.astype(jnp.bfloat16)
        d_in_w = jnp.dot(normed_b.T, d_proj_b, preferred_element_type=jnp.float32)
        d_normed = jnp.dot(d_proj_b, in_weight.T, preferred_element_type=jnp.float32)
        d_resid, d_gain = norm_back(d_normed)
        grad_rows = cots.astype(jnp.float32) + d_resid
        terms = (d_gain, d_in_w, d_cw, d_cb, d_sb, d_dl, d_sk, d_mg, d_out_w)
        return (tuple((left + right for left, right in zip(carry, terms))), (out_rows, grad_rows))
    start = (jnp.zeros((D,), jnp.float32), jnp.zeros((D, PROJ), jnp.float32), jnp.zeros((KCONV, CONV_CH), jnp.float32), jnp.zeros((CONV_CH,), jnp.float32), jnp.zeros((NH,), jnp.float32), jnp.zeros((NH,), jnp.float32), jnp.zeros((NH,), jnp.float32), jnp.zeros((DI,), jnp.float32), jnp.zeros((DI, D), jnp.float32))
    grads, (out_all, grad_all) = lax.scan(one_seq, start, (rows_all, cots_all, lengths))
    g_gain, g_in, g_cw, g_cb, g_sb, g_dl, g_sk, g_mg, g_out = grads
    return (out_all.reshape(TOKENS, D), grad_all.reshape(TOKENS, D), g_gain, g_in, g_cw, g_cb, g_sb, g_dl, g_sk, g_mg, g_out)
```

```python
import jax
import jax.numpy as jnp
from jax import lax
from jax.experimental import pallas as pl
from jax.experimental.pallas import tpu as pltpu
from jax.sharding import PartitionSpec as P

NH = 24
HD = 64
NS = 128
KCONV = 4
DI = 1536
CONV_CH = 1792
PROJ = 3352
LANES = 128
PAIR = LANES // HD
CUTS = (0, 1152, 2304, PROJ)

EPS = 1e-05
HIGH = lax.Precision.HIGHEST


def pre_norm(rows, gain):
    scale = lax.rsqrt(jnp.mean(rows * rows, axis=-1, keepdims=True) + EPS)
    return rows * scale * gain


def contract(left, right, left_dim, right_dim, precision=None):
    return lax.dot_general(
        left,
        right,
        (((left_dim,), (right_dim,)), ((), ())),
        precision=precision,
        preferred_element_type=jnp.float32,
    )


def column_of(array, head):
    lane = lax.broadcasted_iota(jnp.int32, array.shape, 1)
    return jnp.sum(jnp.where(lane == head, array, 0.0), axis=1, keepdims=True)


def tiles_of(length):
    half = length // 2
    return half, ((0, 0), (1, 0), (1, 1))


def decay_tile(cum_col, cum_row, half, row, col):
    spread = cum_col[row * half : (row + 1) * half] - cum_row[:, col * half : (col + 1) * half]
    if row == col:
        rows = lax.broadcasted_iota(jnp.int32, spread.shape, 0)
        cols = lax.broadcasted_iota(jnp.int32, spread.shape, 1)
        spread = jnp.where(rows >= cols, spread, -jnp.inf)
    return jnp.exp(spread)


def pair_lanes(shape):
    return lax.broadcasted_iota(jnp.int32, shape, 1) // HD


def scan_fwd_kernel(x_ref, dt_ref, cum_ref, cumt_ref, b_ref, c_ref, y_ref, score):
    pair = pl.program_id(0)
    length = x_ref.shape[0]
    half, tiles = tiles_of(length)

    @pl.when(pair == 0)
    def _():
        score[...] = contract(c_ref[...], b_ref[...], 1, 1, HIGH)

    which = pair_lanes(x_ref.shape)
    x = x_ref[...]
    sums = [None, None]
    for sub in range(PAIR):
        head = pair * PAIR + sub
        cum_col = column_of(cum_ref[...], head)
        cum_row = cumt_ref[pl.ds(head, 1), :]
        scaled = jnp.where(which == sub, x * column_of(dt_ref[...], head), 0.0)
        scaled = scaled.astype(jnp.bfloat16)
        for row, col in tiles:
            decay = decay_tile(cum_col, cum_row, half, row, col)
            part = score[row * half : (row + 1) * half, col * half : (col + 1) * half]
            mixed = (part * decay).astype(jnp.bfloat16)
            term = contract(mixed, scaled[col * half : (col + 1) * half], 1, 0)
            sums[row] = term if sums[row] is None else sums[row] + term
    for row in range(2):
        y_ref[row * half : (row + 1) * half, :] = sums[row]


def scan_bwd_kernel(
    x_ref, dt_ref, cum_ref, cumt_ref, b_ref, c_ref, dy_ref,
    dx_ref, ddt_ref, drow_ref, dcol_ref, db_ref, dc_ref, score, dscore,
):
    pair = pl.program_id(0)
    length = x_ref.shape[0]
    half, tiles = tiles_of(length)

    @pl.when(pair == 0)
    def _():
        score[...] = contract(c_ref[...], b_ref[...], 1, 1, HIGH)
        dscore[...] = jnp.zeros_like(dscore)
        ddt_ref[...] = jnp.zeros_like(ddt_ref)
        drow_ref[...] = jnp.zeros_like(drow_ref)

    which = pair_lanes(x_ref.shape)
    lane = lax.broadcasted_iota(jnp.int32, x_ref.shape, 1)
    x = x_ref[...]
    dy = dy_ref[...]
    d_scaled = [None, None]
    dt_pair = jnp.zeros_like(x)
    for sub in range(PAIR):
        head = pair * PAIR + sub
        cum_col = column_of(cum_ref[...], head)
        cum_row = cumt_ref[pl.ds(head, 1), :]
        dt_here = jnp.where(which == sub, column_of(dt_ref[...], head), 0.0)
        dt_pair = dt_pair + dt_here
        scaled = (x * dt_here).astype(jnp.bfloat16)
        dy_here = jnp.where(which == sub, dy, 0.0).astype(jnp.bfloat16)
        row_sum = [None, None]
        col_sum = [None, None]
        for row, col in tiles:
            rows = slice(row * half, (row + 1) * half)
            cols = slice(col * half, (col + 1) * half)
            decay = decay_tile(cum_col, cum_row, half, row, col)
            part = score[rows, cols]
            mixed = (part * decay).astype(jnp.bfloat16)
            d_mixed = contract(dy_here[rows], scaled[cols], 1, 1) * decay
            dscore[rows, cols] += d_mixed
            weight = d_mixed * part
            over_cols = jnp.sum(weight, axis=1, keepdims=True)
            over_rows = jnp.sum(weight, axis=0, keepdims=True)
            term = contract(mixed, dy_here[rows], 0, 0)
            row_sum[row] = over_cols if row_sum[row] is None else row_sum[row] + over_cols
            col_sum[col] = over_rows if col_sum[col] is None else col_sum[col] + over_rows
            d_scaled[col] = term if d_scaled[col] is None else d_scaled[col] + term
        for part_index in range(2):
            span = slice(part_index * half, (part_index + 1) * half)
            drow_ref[span, :] = jnp.where(lane[span] == head, row_sum[part_index], drow_ref[span, :])
            dcol_ref[pl.ds(head, 1), span] = col_sum[part_index]
    for part_index in range(2):
        span = slice(part_index * half, (part_index + 1) * half)
        dx_ref[span, :] = d_scaled[part_index] * dt_pair[span]
        products = d_scaled[part_index] * x[span]
        for sub in range(PAIR):
            head = pair * PAIR + sub
            total = jnp.sum(
                jnp.where(which[span] == sub, products, 0.0), axis=1, keepdims=True
            )
            ddt_ref[span, :] = jnp.where(lane[span] == head, total, ddt_ref[span, :])

    @pl.when(pair == pl.num_programs(0) - 1)
    def _():
        dc_ref[...] = contract(dscore[...], b_ref[...], 1, 0, HIGH)
        db_ref[...] = contract(dscore[...], c_ref[...], 0, 0, HIGH)


def whole_spec(shape):
    return pl.BlockSpec(shape, lambda pair: (0, 0))


def scan_operands(x, dt, cum):
    pad = ((0, 0), (0, LANES - NH))
    return x, jnp.pad(dt, pad), jnp.pad(cum, pad), cum.T


def scan_specs(length):
    lanes = whole_spec((length, LANES))
    return [
        pl.BlockSpec((length, LANES), lambda pair: (0, pair)),
        lanes,
        lanes,
        whole_spec((NH, length)),
        whole_spec((length, NS)),
        whole_spec((length, NS)),
    ]


@jax.custom_vjp
def span_scan(x, dt, cum, keys_b, query_c):
    length = x.shape[0]
    return pl.pallas_call(
        scan_fwd_kernel,
        grid=(NH // PAIR,),
        in_specs=scan_specs(length),
        out_specs=pl.BlockSpec((length, LANES), lambda pair: (0, pair)),
        out_shape=jax.ShapeDtypeStruct(x.shape, jnp.float32),
        scratch_shapes=[pltpu.VMEM((length, length), jnp.float32)],
        name="scan_fwd",
    )(*scan_operands(x, dt, cum), keys_b, query_c)


def span_scan_fwd(x, dt, cum, keys_b, query_c):
    return span_scan(x, dt, cum, keys_b, query_c), (x, dt, cum, keys_b, query_c)


def span_scan_bwd(saved, dy):
    x, dt, cum, keys_b, query_c = saved
    length = x.shape[0]
    pair_block = pl.BlockSpec((length, LANES), lambda pair: (0, pair))
    lanes = whole_spec((length, LANES))
    square = pltpu.VMEM((length, length), jnp.float32)
    f32 = jnp.float32
    dx, ddt, drow, dcol, db, dc = pl.pallas_call(
        scan_bwd_kernel,
        grid=(NH // PAIR,),
        in_specs=scan_specs(length) + [pair_block],
        out_specs=[
            pair_block, lanes, lanes, whole_spec((NH, length)),
            whole_spec((length, NS)), whole_spec((length, NS)),
        ],
        out_shape=[
            jax.ShapeDtypeStruct(x.shape, f32),
            jax.ShapeDtypeStruct((length, LANES), f32),
            jax.ShapeDtypeStruct((length, LANES), f32),
            jax.ShapeDtypeStruct((NH, length), f32),
            jax.ShapeDtypeStruct((length, NS), f32),
            jax.ShapeDtypeStruct((length, NS), f32),
        ],
        scratch_shapes=[square, square],
        name="scan_bwd",
    )(*scan_operands(x, dt, cum), keys_b, query_c, dy)
    return dx, ddt[:, :NH], drow[:, :NH] - dcol.T, db, dc


span_scan.defvjp(span_scan_fwd, span_scan_bwd)


def mixer_core(proj, conv_w, conv_b, step_bias, decay_log, skip_weight, mix_gain):
    length = proj.shape[0]
    gate = proj[:, :DI]
    conv_in = proj[:, DI : DI + CONV_CH]
    step_raw = proj[:, DI + CONV_CH :]
    padded = jnp.pad(conv_in, ((KCONV - 1, 0), (0, 0)))
    conv_out = jnp.zeros_like(conv_in) + conv_b
    for offset in range(KCONV):
        conv_out = conv_out + conv_w[offset] * padded[offset : offset + length]
    active = jax.nn.silu(conv_out)
    values = active[:, :DI]
    keys_b = active[:, DI : DI + NS]
    query_c = active[:, DI + NS :]
    step = jax.nn.softplus(step_raw + step_bias)
    logdecay = -step * jnp.exp(decay_log)
    causal = (jnp.arange(length)[:, None] >= jnp.arange(length)[None, :]).astype(jnp.float32)
    cum = jnp.dot(causal, logdecay, precision=HIGH)
    mixed = span_scan(values, step, cum, keys_b, query_c)
    mixed = mixed + jnp.repeat(skip_weight, HD) * values
    flat = mixed * jax.nn.silu(gate)
    scale = lax.rsqrt(jnp.mean(flat * flat, axis=-1, keepdims=True) + EPS)
    return flat * scale * mix_gain


def bits_of(axis):
    size = lax.axis_size(axis)
    return [(axis, 1 << k) for k in reversed(range(size.bit_length() - 1))]


def swap(array, label):
    axis, bit = label
    size = lax.axis_size(axis)
    return lax.ppermute(array, axis, [(i, i ^ bit) for i in range(size)])


def my_bit(label):
    return (lax.axis_index(label[0]) // label[1]) % 2


def orders():
    fsdp, rep = bits_of("fsdp"), bits_of("rep")
    near, wide = fsdp[-1:], fsdp[:-1]
    mid, far = wide[-1:], wide[:-1]
    core, row = rep[-1:], rep[:-1]
    return (
        core + row + near + mid + far,
        core + near + mid + row + far,
        core + mid + row + near + far,
    )


def halve(grad, order):
    labels = bits_of("fsdp") + bits_of("rep")
    grad = grad.reshape((2,) * len(labels) + (-1, grad.shape[-1]))
    for label in order:
        dim = labels.index(label)
        bit = my_bit(label)
        away = lax.dynamic_index_in_dim(grad, 1 - bit, dim, keepdims=False)
        keep = lax.dynamic_index_in_dim(grad, bit, dim, keepdims=False)
        grad = keep + swap(away.astype(jnp.bfloat16), label).astype(jnp.float32)
        labels.remove(label)
    return grad


def double(piece, order):
    labels = bits_of("fsdp") + bits_of("rep")
    present = []
    tail = piece.shape[1:]
    for label in order:
        other = swap(piece, label)
        place = labels.index(label)
        dim = sum(seen < place for seen in present)
        piece = jnp.where(
            my_bit(label) == 0,
            jnp.stack([piece, other], dim),
            jnp.stack([other, piece], dim),
        )
        present.append(place)
    return piece.reshape((-1,) + tail)


def my_rows(shard):
    count = shard.shape[0] // lax.axis_size("rep")
    return lax.dynamic_slice_in_dim(shard, lax.axis_index("rep") * count, count, 0)


def share_rows(piece):
    return double(piece.astype(jnp.bfloat16), bits_of("rep")).astype(jnp.float32)


def sum_all(array):
    for label in reversed(bits_of("fsdp") + bits_of("rep")):
        array = array + swap(array, label)
    return array


def body(
    hidden_in, cotangent, lengths, norm_gain, in_weight, conv_weight, conv_bias,
    step_bias, decay_log, skip_weight, mix_gain, out_weight,
):
    plan = orders()
    small = jnp.concatenate([norm_gain, conv_weight.reshape(-1), conv_bias, mix_gain])
    small = double(small[None], bits_of("fsdp"))
    groups = small.shape[0]
    ends = [norm_gain.size, conv_weight.size, conv_bias.size]
    cut_a, cut_b, cut_c = ends[0], ends[0] + ends[1], sum(ends)
    gain_full = small[:, :cut_a].reshape(-1)
    conv_full = small[:, cut_a:cut_b].reshape(groups, KCONV, -1).transpose(1, 0, 2)
    conv_full = conv_full.reshape(KCONV, -1)
    bias_full = small[:, cut_b:cut_c].reshape(-1)
    mix_full = small[:, cut_c:].reshape(-1)
    in_rows = my_rows(in_weight)
    in_full = jnp.concatenate(
        [
            double(in_rows[:, CUTS[k] : CUTS[k + 1]], plan[k][::-1])
            for k in range(len(CUTS) - 1)
        ],
        axis=1,
    )
    out_full = double(my_rows(out_weight), plan[0][::-1])

    seq_count = lengths.shape[0]
    rows_here = hidden_in.shape[0]
    length = rows_here // seq_count

    def core(proj, *params):
        parts = [
            mixer_core(proj[s * length : (s + 1) * length], *params) for s in range(seq_count)
        ]
        return parts[0] if seq_count == 1 else jnp.concatenate(parts)

    resid = hidden_in.astype(jnp.float32)
    normed, norm_back = jax.vjp(pre_norm, resid, gain_full.astype(jnp.float32))
    normed_b = normed.astype(jnp.bfloat16)
    proj = jnp.dot(normed_b, in_full, preferred_element_type=jnp.float32)
    gated, core_back = jax.vjp(
        core,
        proj,
        conv_full.astype(jnp.float32),
        bias_full.astype(jnp.float32),
        step_bias,
        decay_log,
        skip_weight,
        mix_full.astype(jnp.float32),
    )
    gated_b = gated.astype(jnp.bfloat16)
    branch = jnp.dot(gated_b, out_full, preferred_element_type=jnp.float32)
    live = (
        (jnp.arange(length)[None, :] < lengths[:, None]).reshape(rows_here, 1).astype(jnp.float32)
    )
    block_out = (resid + live * branch).astype(jnp.bfloat16)
    cot_live = cotangent * live.astype(jnp.bfloat16)
    d_out_w = contract(gated_b, cot_live, 0, 0)
    g_out = share_rows(halve(d_out_w, plan[1]))
    d_gated = contract(cot_live, out_full, 1, 1)
    d_proj, d_cw, d_cb, d_sb, d_dl, d_sk, d_mg = core_back(d_gated)
    d_proj_b = d_proj.astype(jnp.bfloat16)
    g_in = jnp.concatenate(
        [
            share_rows(halve(contract(normed_b, d_proj_b[:, CUTS[k] : CUTS[k + 1]], 0, 0), plan[k]))
            for k in range(len(CUTS) - 1)
        ],
        axis=1,
    )
    d_normed = contract(d_proj_b, in_full, 1, 1)
    d_resid, d_gain = norm_back(d_normed)
    grad_in = cotangent.astype(jnp.float32) + d_resid

    vectors = [d_gain, d_cw.reshape(-1), d_cb, d_mg, d_sb, d_dl, d_sk]
    packed = jnp.concatenate(vectors)
    packed = sum_all(jnp.pad(packed, (0, -packed.size % 1024)).reshape(-1, 128)).reshape(-1)
    totals = []
    at = 0
    for vector in vectors:
        totals.append(packed[at : at + vector.size])
        at += vector.size
    me = lax.axis_index("fsdp")

    def mine(array, dim):
        count = array.shape[dim] // groups
        return lax.dynamic_slice_in_dim(array, me * count, count, dim)

    g_gain = mine(totals[0], 0)
    g_cw = mine(totals[1].reshape(KCONV, -1), 1)
    g_cb = mine(totals[2], 0)
    g_mg = mine(totals[3], 0)
    g_sb, g_dl, g_sk = totals[4:]
    return (block_out, grad_in, g_gain, g_in, g_cw, g_cb, g_sb, g_dl, g_sk, g_mg, g_out)


def solution(mesh):
    in_specs = (
        P(("fsdp", "rep"), None),
        P(("fsdp", "rep"), None),
        P(("fsdp", "rep")),
        P("fsdp"),
        P("fsdp", None),
        P(None, "fsdp"),
        P("fsdp"),
        P(),
        P(),
        P(),
        P("fsdp"),
        P("fsdp", None),
    )
    out_specs = (
        P(("fsdp", "rep"), None),
        P(("fsdp", "rep"), None),
        P("fsdp"),
        P("fsdp", None),
        P(None, "fsdp"),
        P("fsdp"),
        P(),
        P(),
        P(),
        P("fsdp"),
        P("fsdp", None),
    )
    return jax.shard_map(body, mesh=mesh, in_specs=in_specs, out_specs=out_specs, check_vma=False)
```

```python
import functools


import jax
import jax.numpy as jnp
from jax import lax
from jax.experimental import pallas as pl
from jax.experimental.pallas import tpu as pltpu
from jax.sharding import PartitionSpec as P

NH = 24
HD = 64
NS = 128
KCONV = 4
DI = 1536
CONV_CH = 1792
PROJ = 3352
LANES = 128
PAIR = LANES // HD
CUTS = (0, 1152, 2304, PROJ)

EPS = 1e-05
HIGH = lax.Precision.HIGHEST


def pre_norm(rows, gain):
    scale = lax.rsqrt(jnp.mean(rows * rows, axis=-1, keepdims=True) + EPS)
    return rows * scale * gain


def contract(left, right, left_dim, right_dim, precision=None):
    return lax.dot_general(
        left,
        right,
        (((left_dim,), (right_dim,)), ((), ())),
        precision=precision,
        preferred_element_type=jnp.float32,
    )


def column_of(array, head):
    lane = lax.broadcasted_iota(jnp.int32, array.shape, 1)
    return jnp.sum(jnp.where(lane == head, array, 0.0), axis=1, keepdims=True)


def tiles_of(length):
    half = length // 2
    return half, ((0, 0), (1, 0), (1, 1))


def decay_tile(cum_col, cum_row, half, row, col):
    spread = cum_col[row * half : (row + 1) * half] - cum_row[:, col * half : (col + 1) * half]
    if row == col:
        rows = lax.broadcasted_iota(jnp.int32, spread.shape, 0)
        cols = lax.broadcasted_iota(jnp.int32, spread.shape, 1)
        spread = jnp.where(rows >= cols, spread, -jnp.inf)
    return jnp.exp(spread)


def pair_lanes(shape):
    return lax.broadcasted_iota(jnp.int32, shape, 1) // HD


def scan_fwd_kernel(x_ref, dt_ref, cum_ref, cumt_ref, b_ref, c_ref, y_ref, score):
    pair = pl.program_id(0)
    length = x_ref.shape[0]
    half, tiles = tiles_of(length)

    @pl.when(pair == 0)
    def _():
        score[...] = contract(c_ref[...], b_ref[...], 1, 1, HIGH)

    which = pair_lanes(x_ref.shape)
    x = x_ref[...]
    sums = [None, None]
    for sub in range(PAIR):
        head = pair * PAIR + sub
        cum_col = column_of(cum_ref[...], head)
        cum_row = cumt_ref[pl.ds(head, 1), :]
        scaled = jnp.where(which == sub, x * column_of(dt_ref[...], head), 0.0)
        scaled = scaled.astype(jnp.bfloat16)
        for row, col in tiles:
            decay = decay_tile(cum_col, cum_row, half, row, col)
            part = score[row * half : (row + 1) * half, col * half : (col + 1) * half]
            mixed = (part * decay).astype(jnp.bfloat16)
            term = contract(mixed, scaled[col * half : (col + 1) * half], 1, 0)
            sums[row] = term if sums[row] is None else sums[row] + term
    for row in range(2):
        y_ref[row * half : (row + 1) * half, :] = sums[row]


def scan_bwd_kernel(
    x_ref, dt_ref, cum_ref, cumt_ref, b_ref, c_ref, dy_ref,
    dx_ref, ddt_ref, drow_ref, dcol_ref, db_ref, dc_ref, score, dscore,
):
    pair = pl.program_id(0)
    length = x_ref.shape[0]
    half, tiles = tiles_of(length)

    @pl.when(pair == 0)
    def _():
        score[...] = contract(c_ref[...], b_ref[...], 1, 1, HIGH)
        dscore[...] = jnp.zeros_like(dscore)
        ddt_ref[...] = jnp.zeros_like(ddt_ref)
        drow_ref[...] = jnp.zeros_like(drow_ref)

    which = pair_lanes(x_ref.shape)
    lane = lax.broadcasted_iota(jnp.int32, x_ref.shape, 1)
    x = x_ref[...]
    dy = dy_ref[...]
    d_scaled = [None, None]
    dt_pair = jnp.zeros_like(x)
    for sub in range(PAIR):
        head = pair * PAIR + sub
        cum_col = column_of(cum_ref[...], head)
        cum_row = cumt_ref[pl.ds(head, 1), :]
        dt_here = jnp.where(which == sub, column_of(dt_ref[...], head), 0.0)
        dt_pair = dt_pair + dt_here
        scaled = (x * dt_here).astype(jnp.bfloat16)
        dy_here = jnp.where(which == sub, dy, 0.0).astype(jnp.bfloat16)
        row_sum = [None, None]
        col_sum = [None, None]
        for row, col in tiles:
            rows = slice(row * half, (row + 1) * half)
            cols = slice(col * half, (col + 1) * half)
            decay = decay_tile(cum_col, cum_row, half, row, col)
            part = score[rows, cols]
            mixed = (part * decay).astype(jnp.bfloat16)
            d_mixed = contract(dy_here[rows], scaled[cols], 1, 1) * decay
            dscore[rows, cols] += d_mixed
            weight = d_mixed * part
            over_cols = jnp.sum(weight, axis=1, keepdims=True)
            over_rows = jnp.sum(weight, axis=0, keepdims=True)
            term = contract(mixed, dy_here[rows], 0, 0)
            row_sum[row] = over_cols if row_sum[row] is None else row_sum[row] + over_cols
            col_sum[col] = over_rows if col_sum[col] is None else col_sum[col] + over_rows
            d_scaled[col] = term if d_scaled[col] is None else d_scaled[col] + term
        for part_index in range(2):
            span = slice(part_index * half, (part_index + 1) * half)
            drow_ref[span, :] = jnp.where(lane[span] == head, row_sum[part_index], drow_ref[span, :])
            dcol_ref[pl.ds(head, 1), span] = col_sum[part_index]
    for part_index in range(2):
        span = slice(part_index * half, (part_index + 1) * half)
        dx_ref[span, :] = d_scaled[part_index] * dt_pair[span]
        products = d_scaled[part_index] * x[span]
        for sub in range(PAIR):
            head = pair * PAIR + sub
            total = jnp.sum(
                jnp.where(which[span] == sub, products, 0.0), axis=1, keepdims=True
            )
            ddt_ref[span, :] = jnp.where(lane[span] == head, total, ddt_ref[span, :])

    @pl.when(pair == pl.num_programs(0) - 1)
    def _():
        dc_ref[...] = contract(dscore[...], b_ref[...], 1, 0, HIGH)
        db_ref[...] = contract(dscore[...], c_ref[...], 0, 0, HIGH)


def whole_spec(shape):
    return pl.BlockSpec(shape, lambda pair: (0, 0))


def scan_operands(x, dt, cum):
    pad = ((0, 0), (0, LANES - NH))
    return x, jnp.pad(dt, pad), jnp.pad(cum, pad), cum.T


def scan_specs(length):
    lanes = whole_spec((length, LANES))
    return [
        pl.BlockSpec((length, LANES), lambda pair: (0, pair)),
        lanes,
        lanes,
        whole_spec((NH, length)),
        whole_spec((length, NS)),
        whole_spec((length, NS)),
    ]


@jax.custom_vjp
def span_scan(x, dt, cum, keys_b, query_c):
    length = x.shape[0]
    return pl.pallas_call(
        scan_fwd_kernel,
        grid=(NH // PAIR,),
        in_specs=scan_specs(length),
        out_specs=pl.BlockSpec((length, LANES), lambda pair: (0, pair)),
        out_shape=jax.ShapeDtypeStruct(x.shape, jnp.float32),
        scratch_shapes=[pltpu.VMEM((length, length), jnp.float32)],
        name="scan_fwd",
    )(*scan_operands(x, dt, cum), keys_b, query_c)


def span_scan_fwd(x, dt, cum, keys_b, query_c):
    return span_scan(x, dt, cum, keys_b, query_c), (x, dt, cum, keys_b, query_c)


def span_scan_bwd(saved, dy):
    x, dt, cum, keys_b, query_c = saved
    length = x.shape[0]
    pair_block = pl.BlockSpec((length, LANES), lambda pair: (0, pair))
    lanes = whole_spec((length, LANES))
    square = pltpu.VMEM((length, length), jnp.float32)
    f32 = jnp.float32
    dx, ddt, drow, dcol, db, dc = pl.pallas_call(
        scan_bwd_kernel,
        grid=(NH // PAIR,),
        in_specs=scan_specs(length) + [pair_block],
        out_specs=[
            pair_block, lanes, lanes, whole_spec((NH, length)),
            whole_spec((length, NS)), whole_spec((length, NS)),
        ],
        out_shape=[
            jax.ShapeDtypeStruct(x.shape, f32),
            jax.ShapeDtypeStruct((length, LANES), f32),
            jax.ShapeDtypeStruct((length, LANES), f32),
            jax.ShapeDtypeStruct((NH, length), f32),
            jax.ShapeDtypeStruct((length, NS), f32),
            jax.ShapeDtypeStruct((length, NS), f32),
        ],
        scratch_shapes=[square, square],
        name="scan_bwd",
    )(*scan_operands(x, dt, cum), keys_b, query_c, dy)
    return dx, ddt[:, :NH], drow[:, :NH] - dcol.T, db, dc


span_scan.defvjp(span_scan_fwd, span_scan_bwd)


def mixer_core(proj, conv_w, conv_b, step_bias, decay_log, skip_weight, mix_gain):
    length = proj.shape[0]
    gate = proj[:, :DI]
    conv_in = proj[:, DI : DI + CONV_CH]
    step_raw = proj[:, DI + CONV_CH :]
    padded = jnp.pad(conv_in, ((KCONV - 1, 0), (0, 0)))
    conv_out = jnp.zeros_like(conv_in) + conv_b
    for offset in range(KCONV):
        conv_out = conv_out + conv_w[offset] * padded[offset : offset + length]
    active = jax.nn.silu(conv_out)
    values = active[:, :DI]
    keys_b = active[:, DI : DI + NS]
    query_c = active[:, DI + NS :]
    step = jax.nn.softplus(step_raw + step_bias)
    logdecay = -step * jnp.exp(decay_log)
    causal = (jnp.arange(length)[:, None] >= jnp.arange(length)[None, :]).astype(jnp.float32)
    cum = jnp.dot(causal, logdecay, precision=HIGH)
    mixed = span_scan(values, step, cum, keys_b, query_c)
    mixed = mixed + jnp.repeat(skip_weight, HD) * values
    flat = mixed * jax.nn.silu(gate)
    scale = lax.rsqrt(jnp.mean(flat * flat, axis=-1, keepdims=True) + EPS)
    return flat * scale * mix_gain


def bits_of(axis):
    size = lax.axis_size(axis)
    return [(axis, 1 << k) for k in reversed(range(size.bit_length() - 1))]


def all_labels():
    return bits_of("fsdp") + bits_of("rep")


def my_bit(label):
    return (lax.axis_index(label[0]) // label[1]) % 2


def partner(label):
    ids = {name: lax.axis_index(name) for name in ("fsdp", "rep")}
    ids[label[0]] = ids[label[0]] + label[1] * (1 - 2 * my_bit(label))
    return (ids["fsdp"], ids["rep"])


def greet(labels):
    barrier = pltpu.get_barrier_semaphore()
    for label in labels:
        pl.semaphore_signal(
            barrier, inc=1, device_id=partner(label), device_id_type=pl.DeviceIdType.MESH
        )
    pl.semaphore_wait(barrier, len(labels))


def send(source, target, sems, stream, slot, label):
    copy = pltpu.make_async_remote_copy(
        src_ref=source,
        dst_ref=target,
        send_sem=sems[0].at[stream, slot],
        recv_sem=sems[1].at[stream, slot],
        device_id=partner(label),
        device_id_type=pl.DeviceIdType.MESH,
    )
    copy.start()
    return copy


def orders():
    fsdp, rep = bits_of("fsdp"), bits_of("rep")
    near, wide = fsdp[-1:], fsdp[:-1]
    mid, far = wide[-1:], wide[:-1]
    core, row = rep[-1:], rep[:-1]
    return (
        core + row + near + mid + far,
        core + near + mid + row + far,
        core + mid + row + near + far,
    )


def position(order):
    place = 0
    for label in order:
        place = place * 2 + my_bit(label)
    return place


def gather_kernel(plan, *refs):
    count = len(plan)
    ins, outs = refs[:count], refs[count : 2 * count]
    sems, local = refs[2 * count : 2 * count + 2], refs[2 * count + 2]
    greet(all_labels())
    steps = max(len(order) for order in plan)
    open_sends, waiting, locals_ = [], {}, []
    for k in range(count):
        copy = pltpu.make_async_copy(ins[k], outs[k].at[pl.ds(position(plan[k]), 1)], local.at[k])
        copy.start()
        locals_.append(copy)
    for step in range(steps):
        for k, order in enumerate(plan):
            if step >= len(order):
                continue
            size = 1 << step
            start = position(order) // size * size
            if step == 0:
                source = ins[k]
            else:
                if step == 1:
                    locals_[k].wait()
                waiting[k].wait_recv()
                source = outs[k].at[pl.ds(start, size)]
            label = order[len(order) - 1 - step]
            copy = send(source, outs[k].at[pl.ds(start, size)], sems, k, step, label)
            waiting[k] = copy
            open_sends.append(copy)
    for k in range(count):
        waiting[k].wait_recv()
        if len(plan[k]) < 2:
            locals_[k].wait()
    for copy in open_sends:
        copy.wait_send()


def gather_all(plan, pieces):
    steps = max(len(order) for order in plan)
    vmem = pl.BlockSpec(memory_space=pltpu.VMEM)
    return pl.pallas_call(
        functools.partial(gather_kernel, plan),
        in_specs=[vmem] * len(pieces),
        out_specs=[vmem] * len(pieces),
        out_shape=[
            jax.ShapeDtypeStruct((1 << len(order),) + piece.shape[1:], piece.dtype)
            for order, piece in zip(plan, pieces)
        ],
        scratch_shapes=[
            pltpu.SemaphoreType.DMA((len(pieces), steps)),
            pltpu.SemaphoreType.DMA((len(pieces), steps)),
            pltpu.SemaphoreType.DMA((len(pieces),)),
        ],
        compiler_params=pltpu.CompilerParams(
            collective_id=0, has_side_effects=True, vmem_limit_bytes=60 << 20
        ),
        name="gather_weights",
    )(*pieces)


def reduce_kernel(plan, tail, *refs):
    count = len(plan)
    steps = len(plan[0])
    grads, vector = refs[:count], refs[count]
    outs, total = refs[count + 1 : 2 * count + 1], refs[2 * count + 1]
    at = 2 * count + 2
    held = [refs[at + k * steps : at + (k + 1) * steps] for k in range(count)]
    at += count * steps
    sums = refs[at : at + steps]
    sems, local = refs[at + steps : at + steps + 2], refs[at + steps + 2]
    labels = all_labels()
    greet(labels)
    open_sends, waiting = [], {}
    vector_order = labels[::-1]

    def source_of(k, step):
        return grads[k] if step == 0 else held[k][step - 1]

    def add_in(k, step):
        size = 1 << (steps - 1 - step)
        base = source_of(k, step)
        target = held[k][step]
        start = my_bit(plan[k][step]) * size

        def one(i, carry):
            left = base[start + i].astype(jnp.float32)
            target[i] = (left + target[i].astype(jnp.float32)).astype(target.dtype)
            return carry

        lax.fori_loop(0, size, one, 0)

    for step in range(steps):
        for k in range(count):
            if step > 0:
                waiting[k].wait_recv()
                add_in(k, step - 1)
            label = plan[k][step]
            size = 1 << (steps - 1 - step)
            away = source_of(k, step).at[pl.ds((1 - my_bit(label)) * size, size)]
            waiting[k] = send(away, held[k][step], sems, k, step, label)
            open_sends.append(waiting[k])
        if step > 0:
            waiting[count].wait_recv()
            before = vector if step == 1 else sums[step - 2]
            sums[step - 1][...] = before[...] + sums[step - 1][...]
        now = vector if step == 0 else sums[step - 1]
        waiting[count] = send(now, sums[step], sems, count, step, vector_order[step])
        open_sends.append(waiting[count])

    here = lax.axis_index("rep")
    known = {k: [0] for k in range(count)}
    inbox = {k: [] for k in range(count)}
    for hop, label in enumerate(tail):
        for k in range(count):
            if hop == 0:
                waiting[k].wait_recv()
                add_in(k, steps - 1)
                copy = pltpu.make_async_copy(
                    held[k][steps - 1], outs[k].at[pl.ds(here, 1)], local.at[k]
                )
                copy.start()
                waiting[k] = copy
            for copy in inbox[k]:
                copy.wait_recv()
            inbox[k] = []
            shift = label[1] * (1 - 2 * my_bit(label))
            for n, offset in enumerate(list(known[k])):
                place = pl.ds(here + offset, 1)
                source = held[k][steps - 1] if n == 0 else outs[k].at[place]
                copy = send(source, outs[k].at[place], sems, k, steps + (1 << hop) - 1 + n, label)
                inbox[k].append(copy)
                open_sends.append(copy)
                known[k].append(offset + shift)
    waiting[count].wait_recv()
    before = sums[steps - 2]
    total[...] = before[...] + sums[steps - 1][...]
    for k in range(count):
        for copy in inbox[k]:
            copy.wait_recv()
        waiting[k].wait()
    for copy in open_sends:
        copy.wait_send()


def reduce_all(plan, grads, vector):
    steps = len(plan[0])
    reps = lax.axis_size("rep")
    vmem = pl.BlockSpec(memory_space=pltpu.VMEM)
    slots = pltpu.SemaphoreType.DMA((len(grads) + 1, steps + reps))
    scratch = []
    for grad in grads:
        scratch += [
            pltpu.VMEM((1 << (steps - 1 - step),) + grad.shape[1:], grad.dtype)
            for step in range(steps)
        ]
    scratch += [pltpu.VMEM(vector.shape, vector.dtype) for _ in range(steps)]
    return pl.pallas_call(
        functools.partial(reduce_kernel, plan, bits_of("rep")),
        in_specs=[vmem] * (len(grads) + 1),
        out_specs=[vmem] * (len(grads) + 1),
        out_shape=[jax.ShapeDtypeStruct((reps,) + g.shape[1:], g.dtype) for g in grads]
        + [jax.ShapeDtypeStruct(vector.shape, vector.dtype)],
        scratch_shapes=scratch + [slots, slots, pltpu.SemaphoreType.DMA((len(grads),))],
        compiler_params=pltpu.CompilerParams(
            collective_id=1, has_side_effects=True, vmem_limit_bytes=60 << 20
        ),
        name="reduce_grads",
    )(*grads, vector)


def to_order(array, order):
    labels = all_labels()
    rows = array.shape[0] >> len(labels)
    perm = [labels.index(label) for label in order] + [len(labels), len(labels) + 1]
    split = array.reshape((2,) * len(labels) + (rows, array.shape[1]))
    return split.transpose(perm).reshape((-1, rows, array.shape[1]))


def from_order(blocks, order):
    labels = all_labels()
    perm = [order.index(label) for label in labels] + [len(labels), len(labels) + 1]
    split = blocks.reshape((2,) * len(labels) + blocks.shape[1:])
    return split.transpose(perm).reshape((-1, blocks.shape[-1]))


def my_rows(shard):
    count = shard.shape[0] // lax.axis_size("rep")
    return lax.dynamic_slice_in_dim(shard, lax.axis_index("rep") * count, count, 0)


def body(
    hidden_in, cotangent, lengths, norm_gain, in_weight, conv_weight, conv_bias,
    step_bias, decay_log, skip_weight, mix_gain, out_weight,
):
    plan = orders()
    columns = [slice(CUTS[k], CUTS[k + 1]) for k in range(len(CUTS) - 1)]
    width = out_weight.shape[1] // len(columns)
    out_columns = [slice(k * width, (k + 1) * width) for k in range(len(columns))]
    small = jnp.concatenate([norm_gain, conv_weight.reshape(-1), conv_bias, mix_gain])
    small = jnp.pad(small, (0, -small.size % 2048)).reshape(1, -1, LANES)
    in_rows, out_rows = my_rows(in_weight), my_rows(out_weight)
    pieces = [small] + [in_rows[None, :, cut] for cut in columns]
    pieces += [out_rows[None, :, cut] for cut in out_columns]
    wide_plan = list(plan) + list(plan)
    gathered = gather_all([bits_of("fsdp")] + wide_plan, pieces)
    full = [from_order(blocks, order) for blocks, order in zip(gathered[1:], wide_plan)]
    in_full = jnp.concatenate(full[: len(columns)], axis=1)
    out_full = jnp.concatenate(full[len(columns) :], axis=1)
    small = gathered[0].reshape(lax.axis_size("fsdp"), -1)
    groups = small.shape[0]
    ends = [norm_gain.size, conv_weight.size, conv_bias.size]
    cut_a, cut_b, cut_c = ends[0], ends[0] + ends[1], sum(ends)
    gain_full = small[:, :cut_a].reshape(-1)
    conv_full = small[:, cut_a:cut_b].reshape(groups, KCONV, -1).transpose(1, 0, 2)
    conv_full = conv_full.reshape(KCONV, -1)
    bias_full = small[:, cut_b:cut_c].reshape(-1)
    mix_full = small[:, cut_c : cut_c + mix_gain.size].reshape(-1)

    seq_count = lengths.shape[0]
    rows_here = hidden_in.shape[0]
    length = rows_here // seq_count

    def core(proj, *params):
        parts = [
            mixer_core(proj[s * length : (s + 1) * length], *params) for s in range(seq_count)
        ]
        return parts[0] if seq_count == 1 else jnp.concatenate(parts)

    resid = hidden_in.astype(jnp.float32)
    normed, norm_back = jax.vjp(pre_norm, resid, gain_full.astype(jnp.float32))
    normed_b = normed.astype(jnp.bfloat16)
    proj = jnp.dot(normed_b, in_full, preferred_element_type=jnp.float32)
    gated, core_back = jax.vjp(
        core,
        proj,
        conv_full.astype(jnp.float32),
        bias_full.astype(jnp.float32),
        step_bias,
        decay_log,
        skip_weight,
        mix_full.astype(jnp.float32),
    )
    gated_b = gated.astype(jnp.bfloat16)
    branch = jnp.dot(gated_b, out_full, preferred_element_type=jnp.float32)
    live = (
        (jnp.arange(length)[None, :] < lengths[:, None]).reshape(rows_here, 1).astype(jnp.float32)
    )
    block_out = (resid + live * branch).astype(jnp.bfloat16)
    cot_live = cotangent * live.astype(jnp.bfloat16)
    d_out_w = contract(gated_b, cot_live, 0, 0)
    d_gated = contract(cot_live, out_full, 1, 1)
    d_proj, d_cw, d_cb, d_sb, d_dl, d_sk, d_mg = core_back(d_gated)
    d_proj_b = d_proj.astype(jnp.bfloat16)
    d_normed = contract(d_proj_b, in_full, 1, 1)
    d_resid, d_gain = norm_back(d_normed)
    grad_in = cotangent.astype(jnp.float32) + d_resid

    vectors = [d_gain, d_cw.reshape(-1), d_cb, d_mg, d_sb, d_dl, d_sk]
    packed = jnp.concatenate(vectors)
    packed = jnp.pad(packed, (0, -packed.size % 1024)).reshape(-1, LANES)
    partial = [contract(normed_b, d_proj_b[:, cut], 0, 0) for cut in columns]
    partial += [d_out_w[:, cut] for cut in out_columns]
    blocks = [
        to_order(part.astype(jnp.bfloat16), order) for part, order in zip(partial, wide_plan)
    ]
    *sums, packed = reduce_all(wide_plan, blocks, packed)
    sums = [part.reshape(-1, part.shape[-1]) for part in sums]
    g_in = jnp.concatenate(sums[: len(columns)], axis=1).astype(jnp.float32)
    g_out = jnp.concatenate(sums[len(columns) :], axis=1).astype(jnp.float32)
    packed = packed.reshape(-1)
    totals = []
    at = 0
    for vector in vectors:
        totals.append(packed[at : at + vector.size])
        at += vector.size
    me = lax.axis_index("fsdp")

    def mine(array, dim):
        count = array.shape[dim] // groups
        return lax.dynamic_slice_in_dim(array, me * count, count, dim)

    g_gain = mine(totals[0], 0)
    g_cw = mine(totals[1].reshape(KCONV, -1), 1)
    g_cb = mine(totals[2], 0)
    g_mg = mine(totals[3], 0)
    g_sb, g_dl, g_sk = totals[4:]
    return (block_out, grad_in, g_gain, g_in, g_cw, g_cb, g_sb, g_dl, g_sk, g_mg, g_out)


def solution(mesh):
    in_specs = (
        P(("fsdp", "rep"), None),
        P(("fsdp", "rep"), None),
        P(("fsdp", "rep")),
        P("fsdp"),
        P("fsdp", None),
        P(None, "fsdp"),
        P("fsdp"),
        P(),
        P(),
        P(),
        P("fsdp"),
        P("fsdp", None),
    )
    out_specs = (
        P(("fsdp", "rep"), None),
        P(("fsdp", "rep"), None),
        P("fsdp"),
        P("fsdp", None),
        P(None, "fsdp"),
        P("fsdp"),
        P(),
        P(),
        P(),
        P("fsdp"),
        P("fsdp", None),
    )
    return jax.shard_map(body, mesh=mesh, in_specs=in_specs, out_specs=out_specs, check_vma=False)
```

```python
import functools


import jax
import jax.numpy as jnp
from jax import lax
from jax.experimental import pallas as pl
from jax.experimental.pallas import tpu as pltpu
from jax.sharding import PartitionSpec as P

NH = 24
HD = 64
NS = 128
KCONV = 4
DI = 1536
CONV_CH = 1792
PROJ = 3352
LANES = 128
PAIR = LANES // HD
CUTS = (0, 1152, 2304, PROJ)

EPS = 1e-05
HIGH = lax.Precision.HIGHEST


def pre_norm(rows, gain):
    scale = lax.rsqrt(jnp.mean(rows * rows, axis=-1, keepdims=True) + EPS)
    return rows * scale * gain


def contract(left, right, left_dim, right_dim, precision=None):
    return lax.dot_general(
        left,
        right,
        (((left_dim,), (right_dim,)), ((), ())),
        precision=precision,
        preferred_element_type=jnp.float32,
    )


def column_of(array, head):
    lane = lax.broadcasted_iota(jnp.int32, array.shape, 1)
    return jnp.sum(jnp.where(lane == head, array, 0.0), axis=1, keepdims=True)


def tiles_of(length):
    half = length // 2
    return half, ((0, 0), (1, 0), (1, 1))


def decay_tile(cum_col, cum_row, half, row, col):
    spread = cum_col[row * half : (row + 1) * half] - cum_row[:, col * half : (col + 1) * half]
    if row == col:
        rows = lax.broadcasted_iota(jnp.int32, spread.shape, 0)
        cols = lax.broadcasted_iota(jnp.int32, spread.shape, 1)
        spread = jnp.where(rows >= cols, spread, -jnp.inf)
    return jnp.exp(spread)


def pair_lanes(shape):
    return lax.broadcasted_iota(jnp.int32, shape, 1) // HD


def scan_fwd_kernel(x_ref, dt_ref, cum_ref, cumt_ref, b_ref, c_ref, skip_ref, y_ref, score):
    pair = pl.program_id(0)
    length = x_ref.shape[0]
    half, tiles = tiles_of(length)

    @pl.when(pair == 0)
    def _():
        score[...] = contract(c_ref[...], b_ref[...], 1, 1, HIGH)

    which = pair_lanes(x_ref.shape)
    x = x_ref[...]
    sums = [None, None]
    for sub in range(PAIR):
        head = pair * PAIR + sub
        cum_col = column_of(cum_ref[...], head)
        cum_row = cumt_ref[pl.ds(head, 1), :]
        scaled = jnp.where(which == sub, x * column_of(dt_ref[...], head), 0.0)
        scaled = scaled.astype(jnp.bfloat16)
        for row, col in tiles:
            decay = decay_tile(cum_col, cum_row, half, row, col)
            part = score[row * half : (row + 1) * half, col * half : (col + 1) * half]
            mixed = (part * decay).astype(jnp.bfloat16)
            term = contract(mixed, scaled[col * half : (col + 1) * half], 1, 0)
            sums[row] = term if sums[row] is None else sums[row] + term
    for row in range(2):
        rows = slice(row * half, (row + 1) * half)
        y_ref[rows, :] = sums[row] + skip_ref[...] * x[rows]


def scan_bwd_kernel(
    x_ref, dt_ref, cum_ref, cumt_ref, b_ref, c_ref, skip_ref, dy_ref,
    dx_ref, ddt_ref, drow_ref, dcol_ref, db_ref, dc_ref, dskip_ref, score, dscore,
):
    pair = pl.program_id(0)
    length = x_ref.shape[0]
    half, tiles = tiles_of(length)

    @pl.when(pair == 0)
    def _():
        score[...] = contract(c_ref[...], b_ref[...], 1, 1, HIGH)
        dscore[...] = jnp.zeros_like(dscore)
        ddt_ref[...] = jnp.zeros_like(ddt_ref)
        drow_ref[...] = jnp.zeros_like(drow_ref)

    which = pair_lanes(x_ref.shape)
    lane = lax.broadcasted_iota(jnp.int32, x_ref.shape, 1)
    x = x_ref[...]
    dy = dy_ref[...]
    dskip_ref[...] = jnp.sum(x * dy, axis=0, keepdims=True)
    d_scaled = [None, None]
    dt_pair = jnp.zeros_like(x)
    for sub in range(PAIR):
        head = pair * PAIR + sub
        cum_col = column_of(cum_ref[...], head)
        cum_row = cumt_ref[pl.ds(head, 1), :]
        dt_here = jnp.where(which == sub, column_of(dt_ref[...], head), 0.0)
        dt_pair = dt_pair + dt_here
        scaled = (x * dt_here).astype(jnp.bfloat16)
        dy_here = jnp.where(which == sub, dy, 0.0).astype(jnp.bfloat16)
        row_sum = [None, None]
        col_sum = [None, None]
        for row, col in tiles:
            rows = slice(row * half, (row + 1) * half)
            cols = slice(col * half, (col + 1) * half)
            decay = decay_tile(cum_col, cum_row, half, row, col)
            part = score[rows, cols]
            mixed = (part * decay).astype(jnp.bfloat16)
            d_mixed = contract(dy_here[rows], scaled[cols], 1, 1) * decay
            dscore[rows, cols] += d_mixed
            weight = d_mixed * part
            over_cols = jnp.sum(weight, axis=1, keepdims=True)
            over_rows = jnp.sum(weight, axis=0, keepdims=True)
            term = contract(mixed, dy_here[rows], 0, 0)
            row_sum[row] = over_cols if row_sum[row] is None else row_sum[row] + over_cols
            col_sum[col] = over_rows if col_sum[col] is None else col_sum[col] + over_rows
            d_scaled[col] = term if d_scaled[col] is None else d_scaled[col] + term
        for part_index in range(2):
            span = slice(part_index * half, (part_index + 1) * half)
            drow_ref[span, :] = jnp.where(lane[span] == head, row_sum[part_index], drow_ref[span, :])
            dcol_ref[pl.ds(head, 1), span] = col_sum[part_index]
    for part_index in range(2):
        span = slice(part_index * half, (part_index + 1) * half)
        dx_ref[span, :] = d_scaled[part_index] * dt_pair[span] + skip_ref[...] * dy[span]
        products = d_scaled[part_index] * x[span]
        for sub in range(PAIR):
            head = pair * PAIR + sub
            total = jnp.sum(
                jnp.where(which[span] == sub, products, 0.0), axis=1, keepdims=True
            )
            ddt_ref[span, :] = jnp.where(lane[span] == head, total, ddt_ref[span, :])

    @pl.when(pair == pl.num_programs(0) - 1)
    def _():
        dc_ref[...] = contract(dscore[...], b_ref[...], 1, 0, HIGH)
        db_ref[...] = contract(dscore[...], c_ref[...], 0, 0, HIGH)


def whole_spec(shape):
    return pl.BlockSpec(shape, lambda pair: (0, 0))


def scan_operands(active, dt, cum, skip):
    pad = ((0, 0), (0, LANES - NH))
    return active, jnp.pad(dt, pad), jnp.pad(cum, pad), cum.T, active, active, skip


def scan_specs(length):
    lanes = whole_spec((length, LANES))
    return [
        pl.BlockSpec((length, LANES), lambda pair: (0, pair)),
        lanes,
        lanes,
        whole_spec((NH, length)),
        pl.BlockSpec((length, NS), lambda pair: (0, DI // NS)),
        pl.BlockSpec((length, NS), lambda pair: (0, DI // NS + 1)),
        pl.BlockSpec((1, LANES), lambda pair: (0, pair)),
    ]


@jax.custom_vjp
def span_scan(active, dt, cum, skip):
    length = active.shape[0]
    return pl.pallas_call(
        scan_fwd_kernel,
        grid=(NH // PAIR,),
        in_specs=scan_specs(length),
        out_specs=pl.BlockSpec((length, LANES), lambda pair: (0, pair)),
        out_shape=jax.ShapeDtypeStruct((length, DI), jnp.float32),
        scratch_shapes=[pltpu.VMEM((length, length), jnp.float32)],
        name="scan_fwd",
    )(*scan_operands(active, dt, cum, skip))


def span_scan_fwd(active, dt, cum, skip):
    return span_scan(active, dt, cum, skip), (active, dt, cum, skip)


def span_scan_bwd(saved, dy):
    active, dt, cum, skip = saved
    length = active.shape[0]
    pair_block = pl.BlockSpec((length, LANES), lambda pair: (0, pair))
    lanes = whole_spec((length, LANES))
    square = pltpu.VMEM((length, length), jnp.float32)
    f32 = jnp.float32
    dx, ddt, drow, dcol, db, dc, dskip = pl.pallas_call(
        scan_bwd_kernel,
        grid=(NH // PAIR,),
        in_specs=scan_specs(length) + [pair_block],
        out_specs=[
            pair_block, lanes, lanes, whole_spec((NH, length)),
            whole_spec((length, NS)), whole_spec((length, NS)),
            pl.BlockSpec((1, LANES), lambda pair: (0, pair)),
        ],
        out_shape=[
            jax.ShapeDtypeStruct((length, DI), f32),
            jax.ShapeDtypeStruct((length, LANES), f32),
            jax.ShapeDtypeStruct((length, LANES), f32),
            jax.ShapeDtypeStruct((NH, length), f32),
            jax.ShapeDtypeStruct((length, NS), f32),
            jax.ShapeDtypeStruct((length, NS), f32),
            jax.ShapeDtypeStruct((1, DI), f32),
        ],
        scratch_shapes=[square, square],
        name="scan_bwd",
    )(*scan_operands(active, dt, cum, skip), dy)
    d_active = jnp.concatenate([dx, db, dc], axis=1)
    return d_active, ddt[:, :NH], drow[:, :NH] - dcol.T, dskip


span_scan.defvjp(span_scan_fwd, span_scan_bwd)


def mixer_core(proj, conv_w, conv_b, step_bias, decay_log, skip_weight, mix_gain):
    length = proj.shape[0]
    gate = proj[:, :DI]
    conv_in = proj[:, DI : DI + CONV_CH]
    step_raw = proj[:, DI + CONV_CH :]
    padded = jnp.pad(conv_in, ((KCONV - 1, 0), (0, 0)))
    conv_out = jnp.zeros_like(conv_in) + conv_b
    for offset in range(KCONV):
        conv_out = conv_out + conv_w[offset] * padded[offset : offset + length]
    active = jax.nn.silu(conv_out)
    step = jax.nn.softplus(step_raw + step_bias)
    logdecay = -step * jnp.exp(decay_log)
    causal = (jnp.arange(length)[:, None] >= jnp.arange(length)[None, :]).astype(jnp.float32)
    cum = jnp.dot(causal, logdecay, precision=HIGH)
    mixed = span_scan(active, step, cum, jnp.repeat(skip_weight, HD)[None])
    flat = mixed * jax.nn.silu(gate)
    scale = lax.rsqrt(jnp.mean(flat * flat, axis=-1, keepdims=True) + EPS)
    return flat * scale * mix_gain


def bits_of(axis):
    size = lax.axis_size(axis)
    return [(axis, 1 << k) for k in reversed(range(size.bit_length() - 1))]


def all_labels():
    return bits_of("fsdp") + bits_of("rep")


def my_bit(label):
    return (lax.axis_index(label[0]) // label[1]) % 2


def partner(label):
    ids = {name: lax.axis_index(name) for name in ("fsdp", "rep")}
    ids[label[0]] = ids[label[0]] + label[1] * (1 - 2 * my_bit(label))
    return (ids["fsdp"], ids["rep"])


def greet(labels):
    barrier = pltpu.get_barrier_semaphore()
    for label in labels:
        pl.semaphore_signal(
            barrier, inc=1, device_id=partner(label), device_id_type=pl.DeviceIdType.MESH
        )
    pl.semaphore_wait(barrier, len(labels))


def send(source, target, sems, stream, slot, label):
    copy = pltpu.make_async_remote_copy(
        src_ref=source,
        dst_ref=target,
        send_sem=sems[0].at[stream, slot],
        recv_sem=sems[1].at[stream, slot],
        device_id=partner(label),
        device_id_type=pl.DeviceIdType.MESH,
    )
    copy.start()
    return copy


def orders():
    fsdp, rep = bits_of("fsdp"), bits_of("rep")
    near, wide = fsdp[-1:], fsdp[:-1]
    mid, far = wide[-1:], wide[:-1]
    core, row = rep[-1:], rep[:-1]
    return (
        core + row + near + mid + far,
        core + near + mid + row + far,
        core + mid + row + near + far,
    )


def position(order):
    place = 0
    for label in order:
        place = place * 2 + my_bit(label)
    return place


def gather_kernel(plan, *refs):
    count = len(plan)
    ins, outs = refs[:count], refs[count : 2 * count]
    sems, local = refs[2 * count : 2 * count + 2], refs[2 * count + 2]
    greet(all_labels())
    steps = max(len(order) for order in plan)
    open_sends, waiting, locals_ = [], {}, []
    for k in range(count):
        copy = pltpu.make_async_copy(ins[k], outs[k].at[pl.ds(position(plan[k]), 1)], local.at[k])
        copy.start()
        locals_.append(copy)
    for step in range(steps):
        for k, order in enumerate(plan):
            if step >= len(order):
                continue
            size = 1 << step
            start = position(order) // size * size
            if step == 0:
                source = ins[k]
            else:
                if step == 1:
                    locals_[k].wait()
                waiting[k].wait_recv()
                source = outs[k].at[pl.ds(start, size)]
            label = order[len(order) - 1 - step]
            copy = send(source, outs[k].at[pl.ds(start, size)], sems, k, step, label)
            waiting[k] = copy
            open_sends.append(copy)
    for k in range(count):
        waiting[k].wait_recv()
        if len(plan[k]) < 2:
            locals_[k].wait()
    for copy in open_sends:
        copy.wait_send()


def gather_all(plan, pieces):
    steps = max(len(order) for order in plan)
    vmem = pl.BlockSpec(memory_space=pltpu.VMEM)
    return pl.pallas_call(
        functools.partial(gather_kernel, plan),
        in_specs=[vmem] * len(pieces),
        out_specs=[vmem] * len(pieces),
        out_shape=[
            jax.ShapeDtypeStruct((1 << len(order),) + piece.shape[1:], piece.dtype)
            for order, piece in zip(plan, pieces)
        ],
        scratch_shapes=[
            pltpu.SemaphoreType.DMA((len(pieces), steps)),
            pltpu.SemaphoreType.DMA((len(pieces), steps)),
            pltpu.SemaphoreType.DMA((len(pieces),)),
        ],
        compiler_params=pltpu.CompilerParams(
            collective_id=0, has_side_effects=True, vmem_limit_bytes=60 << 20
        ),
        name="gather_weights",
    )(*pieces)


def reduce_kernel(plan, tail, *refs):
    count = len(plan)
    steps = len(plan[0])
    grads, vector = refs[:count], refs[count]
    outs, total = refs[count + 1 : 2 * count + 1], refs[2 * count + 1]
    at = 2 * count + 2
    held = [refs[at + k * steps : at + (k + 1) * steps] for k in range(count)]
    at += count * steps
    sums = refs[at : at + steps]
    sems, local = refs[at + steps : at + steps + 2], refs[at + steps + 2]
    labels = all_labels()
    greet(labels)
    open_sends, waiting = [], {}
    vector_order = labels[::-1]

    def source_of(k, step):
        return grads[k] if step == 0 else held[k][step - 1]

    def add_in(k, step):
        size = 1 << (steps - 1 - step)
        base = source_of(k, step)
        target = held[k][step]
        start = my_bit(plan[k][step]) * size

        def one(i, carry):
            left = base[start + i].astype(jnp.float32)
            target[i] = (left + target[i].astype(jnp.float32)).astype(target.dtype)
            return carry

        lax.fori_loop(0, size, one, 0)

    for step in range(steps):
        for k in range(count):
            if step > 0:
                waiting[k].wait_recv()
                add_in(k, step - 1)
            label = plan[k][step]
            size = 1 << (steps - 1 - step)
            away = source_of(k, step).at[pl.ds((1 - my_bit(label)) * size, size)]
            waiting[k] = send(away, held[k][step], sems, k, step, label)
            open_sends.append(waiting[k])
        if step > 0:
            waiting[count].wait_recv()
            before = vector if step == 1 else sums[step - 2]
            sums[step - 1][...] = before[...] + sums[step - 1][...]
        now = vector if step == 0 else sums[step - 1]
        waiting[count] = send(now, sums[step], sems, count, step, vector_order[step])
        open_sends.append(waiting[count])

    here = lax.axis_index("rep")
    known = {k: [0] for k in range(count)}
    inbox = {k: [] for k in range(count)}
    for hop, label in enumerate(tail):
        for k in range(count):
            if hop == 0:
                waiting[k].wait_recv()
                add_in(k, steps - 1)
                copy = pltpu.make_async_copy(
                    held[k][steps - 1], outs[k].at[pl.ds(here, 1)], local.at[k]
                )
                copy.start()
                waiting[k] = copy
            for copy in inbox[k]:
                copy.wait_recv()
            inbox[k] = []
            shift = label[1] * (1 - 2 * my_bit(label))
            for n, offset in enumerate(list(known[k])):
                place = pl.ds(here + offset, 1)
                source = held[k][steps - 1] if n == 0 else outs[k].at[place]
                copy = send(source, outs[k].at[place], sems, k, steps + (1 << hop) - 1 + n, label)
                inbox[k].append(copy)
                open_sends.append(copy)
                known[k].append(offset + shift)
    waiting[count].wait_recv()
    before = sums[steps - 2]
    total[...] = before[...] + sums[steps - 1][...]
    for k in range(count):
        for copy in inbox[k]:
            copy.wait_recv()
        waiting[k].wait()
    for copy in open_sends:
        copy.wait_send()


def reduce_all(plan, grads, vector):
    steps = len(plan[0])
    reps = lax.axis_size("rep")
    vmem = pl.BlockSpec(memory_space=pltpu.VMEM)
    slots = pltpu.SemaphoreType.DMA((len(grads) + 1, steps + reps))
    scratch = []
    for grad in grads:
        scratch += [
            pltpu.VMEM((1 << (steps - 1 - step),) + grad.shape[1:], grad.dtype)
            for step in range(steps)
        ]
    scratch += [pltpu.VMEM(vector.shape, vector.dtype) for _ in range(steps)]
    return pl.pallas_call(
        functools.partial(reduce_kernel, plan, bits_of("rep")),
        in_specs=[vmem] * (len(grads) + 1),
        out_specs=[vmem] * (len(grads) + 1),
        out_shape=[jax.ShapeDtypeStruct((reps,) + g.shape[1:], g.dtype) for g in grads]
        + [jax.ShapeDtypeStruct(vector.shape, vector.dtype)],
        scratch_shapes=scratch + [slots, slots, pltpu.SemaphoreType.DMA((len(grads),))],
        compiler_params=pltpu.CompilerParams(
            collective_id=1, has_side_effects=True, vmem_limit_bytes=60 << 20
        ),
        name="reduce_grads",
    )(*grads, vector)


def to_order(array, order):
    labels = all_labels()
    rows = array.shape[0] >> len(labels)
    perm = [labels.index(label) for label in order] + [len(labels), len(labels) + 1]
    split = array.reshape((2,) * len(labels) + (rows, array.shape[1]))
    return split.transpose(perm).reshape((-1, rows, array.shape[1]))


def from_order(blocks, order):
    labels = all_labels()
    perm = [order.index(label) for label in labels] + [len(labels), len(labels) + 1]
    split = blocks.reshape((2,) * len(labels) + blocks.shape[1:])
    return split.transpose(perm).reshape((-1, blocks.shape[-1]))


def whole_lanes(array):
    return jnp.pad(array, ((0, 0), (0, -array.shape[1] % LANES)))


def my_rows(shard):
    count = shard.shape[0] // lax.axis_size("rep")
    return lax.dynamic_slice_in_dim(shard, lax.axis_index("rep") * count, count, 0)


def body(
    hidden_in, cotangent, lengths, norm_gain, in_weight, conv_weight, conv_bias,
    step_bias, decay_log, skip_weight, mix_gain, out_weight,
):
    plan = orders()
    columns = [slice(CUTS[k], CUTS[k + 1]) for k in range(len(CUTS) - 1)]
    width = out_weight.shape[1] // len(columns)
    out_columns = [slice(k * width, (k + 1) * width) for k in range(len(columns))]
    small = jnp.concatenate([norm_gain, conv_weight.reshape(-1), conv_bias, mix_gain])
    small = jnp.pad(small, (0, -small.size % 2048)).reshape(1, -1, LANES)
    in_rows, out_rows = my_rows(in_weight), my_rows(out_weight)
    pieces = [small] + [in_rows[None, :, cut] for cut in columns]
    pieces += [out_rows[None, :, cut] for cut in out_columns]
    wide_plan = list(plan) + list(plan)
    gathered = gather_all([bits_of("fsdp")] + wide_plan, pieces)
    full = [from_order(blocks, order) for blocks, order in zip(gathered[1:], wide_plan)]
    in_full = jnp.concatenate(full[: len(columns)], axis=1)
    out_full = jnp.concatenate(full[len(columns) :], axis=1)
    small = gathered[0].reshape(lax.axis_size("fsdp"), -1)
    groups = small.shape[0]
    ends = [norm_gain.size, conv_weight.size, conv_bias.size]
    cut_a, cut_b, cut_c = ends[0], ends[0] + ends[1], sum(ends)
    gain_full = small[:, :cut_a].reshape(-1)
    conv_full = small[:, cut_a:cut_b].reshape(groups, KCONV, -1).transpose(1, 0, 2)
    conv_full = conv_full.reshape(KCONV, -1)
    bias_full = small[:, cut_b:cut_c].reshape(-1)
    mix_full = small[:, cut_c : cut_c + mix_gain.size].reshape(-1)

    seq_count = lengths.shape[0]
    rows_here = hidden_in.shape[0]
    length = rows_here // seq_count

    def core(proj, *params):
        parts = [
            mixer_core(proj[s * length : (s + 1) * length], *params) for s in range(seq_count)
        ]
        return parts[0] if seq_count == 1 else jnp.concatenate(parts)

    resid = hidden_in.astype(jnp.float32)
    normed, norm_back = jax.vjp(pre_norm, resid, gain_full.astype(jnp.float32))
    normed_b = normed.astype(jnp.bfloat16)
    proj = jnp.dot(normed_b, in_full, preferred_element_type=jnp.float32)
    gated, core_back = jax.vjp(
        core,
        proj,
        conv_full.astype(jnp.float32),
        bias_full.astype(jnp.float32),
        step_bias,
        decay_log,
        skip_weight,
        mix_full.astype(jnp.float32),
    )
    gated_b = gated.astype(jnp.bfloat16)
    branch = jnp.dot(gated_b, out_full, preferred_element_type=jnp.float32)
    live = (
        (jnp.arange(length)[None, :] < lengths[:, None]).reshape(rows_here, 1).astype(jnp.float32)
    )
    block_out = (resid + live * branch).astype(jnp.bfloat16)
    cot_live = cotangent * live.astype(jnp.bfloat16)
    d_out_w = contract(gated_b, cot_live, 0, 0)
    d_gated = contract(cot_live, out_full, 1, 1)
    d_proj, d_cw, d_cb, d_sb, d_dl, d_sk, d_mg = core_back(d_gated)
    d_proj_b = d_proj.astype(jnp.bfloat16)
    d_normed = contract(d_proj_b, in_full, 1, 1)
    d_resid, d_gain = norm_back(d_normed)
    grad_in = cotangent.astype(jnp.float32) + d_resid

    vectors = [d_gain, d_cw.reshape(-1), d_cb, d_mg, d_sb, d_dl, d_sk]
    packed = jnp.concatenate(vectors)
    packed = jnp.pad(packed, (0, -packed.size % 1024)).reshape(-1, LANES)
    partial = [contract(normed_b, whole_lanes(d_proj_b[:, cut]), 0, 0) for cut in columns]
    partial += [d_out_w[:, cut] for cut in out_columns]
    blocks = [
        to_order(part.astype(jnp.bfloat16), order) for part, order in zip(partial, wide_plan)
    ]
    *sums, packed = reduce_all(wide_plan, blocks, packed)
    sums = [part.reshape(-1, part.shape[-1]) for part in sums]
    g_in = jnp.concatenate(sums[: len(columns)], axis=1)[:, :PROJ].astype(jnp.float32)
    g_out = jnp.concatenate(sums[len(columns) :], axis=1).astype(jnp.float32)
    packed = packed.reshape(-1)
    totals = []
    at = 0
    for vector in vectors:
        totals.append(packed[at : at + vector.size])
        at += vector.size
    me = lax.axis_index("fsdp")

    def mine(array, dim):
        count = array.shape[dim] // groups
        return lax.dynamic_slice_in_dim(array, me * count, count, dim)

    g_gain = mine(totals[0], 0)
    g_cw = mine(totals[1].reshape(KCONV, -1), 1)
    g_cb = mine(totals[2], 0)
    g_mg = mine(totals[3], 0)
    g_sb, g_dl, g_sk = totals[4:]
    return (block_out, grad_in, g_gain, g_in, g_cw, g_cb, g_sb, g_dl, g_sk, g_mg, g_out)


def solution(mesh):
    in_specs = (
        P(("fsdp", "rep"), None),
        P(("fsdp", "rep"), None),
        P(("fsdp", "rep")),
        P("fsdp"),
        P("fsdp", None),
        P(None, "fsdp"),
        P("fsdp"),
        P(),
        P(),
        P(),
        P("fsdp"),
        P("fsdp", None),
    )
    out_specs = (
        P(("fsdp", "rep"), None),
        P(("fsdp", "rep"), None),
        P("fsdp"),
        P("fsdp", None),
        P(None, "fsdp"),
        P("fsdp"),
        P(),
        P(),
        P(),
        P("fsdp"),
        P("fsdp", None),
    )
    return jax.shard_map(body, mesh=mesh, in_specs=in_specs, out_specs=out_specs, check_vma=False)
```
